512 devices in a mesh: lat: 32 (over z, y_hi, core), lon: 16 (over y_lo, x).
Axes of the slice: x: 4, y: 8 (y_hi: 2, y_lo: 4; y = y_hi * 4 + y_lo), z: 8, core: 2. Of those that a mesh axis runs over, the one named last changes fastest.
Arguments:
- fields: float32 [5, 32, 32, 4096], P(None, None, 'lat', 'lon'), may hold values from -6 to 6
- east_courant: float32 [32, 32, 4096], P(None, 'lat', 'lon'), may hold values from -0.45 to 0.45
- north_courant: float32 [32, 32, 4096], P(None, 'lat', 'lon'), may hold values from -0.45 to 0.45
- offsets: int32 [32], P('lat'), may hold values from -8 to 7
- lower_blocks: float32 [5, 5, 31, 32], P(None, None, None, 'lat'), may hold values from -0.4 to 0.4
- pivot_inverse: float32 [5, 5, 32, 32], P(None, None, None, 'lat'), may hold values from -0.36 to 1, as said below
- upper_blocks: float32 [5, 5, 31, 32], P(None, None, None, 'lat'), may hold values from -0.4 to 0.4
Outputs:
- solved: float32 [5, 32, 32, 4096], P(None, None, 'lat', 'lon')
The draws below stay inside these ranges and needn't reach their ends.
Inputs may be any that keep to these rules, and one draw needn't show every extreme that they name: `pivot_inverse`: diagonal entries of each 5 x 5 block lie between 0.3 and 1; off-diagonal entries are at most 0.36 in magnitude.
All inputs are finite; a program needn't handle non-finite values.
Results may differ from the reference program's by a relative error of at most 0.0001.
Values sent between devices are 32-bit elements; how exact they have to be, the bound alone decides.
A program may use at most 64 MiB of HBM per device.

```python
import jax
import jax.numpy as jnp
from jax import lax

NF = 5
LEV = 32
LON_DEV = 256
NLAT = 32
NLON = 4096
N_LON = 16


def draw_pivot_inverse(key, part):
    first_key, second_key = jax.random.split(jax.random.fold_in(key, 17))
    shape = (NF, NF, LEV, NLAT)
    diagonal = jax.random.uniform(first_key, shape, jnp.float32, 0.5, 1.0)
    offdiag = 0.12 * jnp.clip(jax.random.normal(second_key, shape, jnp.float32), -3.0, 3.0)
    identity = (jnp.arange(NF)[:, None] == jnp.arange(NF)[None, :])[:, :, None, None]
    return jnp.where(identity, diagonal, offdiag).astype(jnp.float32)


def touch_ends(array, own_key, least, largest):
    spot = [jax.random.randint(jax.random.fold_in(own_key, axis), (), 0, length) for axis, length in enumerate(array.shape)]
    widest = array.shape.index(max(array.shape))
    neighbour = spot[:widest] + [(spot[widest] + 1) % array.shape[widest]] + spot[widest + 1:]
    return array.at[tuple(spot)].set(least).at[tuple(neighbour)].set(largest)


def shard_levels(rng, extent, pieces, least, top_value):
    def one(position, shards_of):
        heights = jax.random.uniform(jax.random.fold_in(jax.random.fold_in(rng, 6), position), (shards_of,), jnp.float32, least / len(pieces), top_value / len(pieces))
        return jnp.repeat(jnp.exp(heights), extent[position] // shards_of).reshape((-1,) + (1,) * (len(extent) - position - 1))

    gain = one(*pieces[0])
    for cut in pieces[1:]:
        gain = gain * one(*cut)
    return gain


def gaussian(key, extent, scale, limit, cuts=(), kind=jnp.bfloat16):
    level = shard_levels(key, extent, cuts, -0.22, 0.18) if cuts else 1.0
    drawn = jax.random.normal(key, extent, jnp.float32) * scale * level
    return jnp.minimum(jnp.maximum(drawn, -limit), limit).astype(kind)


def setup_inputs(seed: int = 0) -> dict:
    key_list = jax.random.split(jax.random.key(seed), 8)
    return {
        "fields": gaussian(key_list[0], (NF, LEV, NLAT, NLON), 1.0, 6.0, ((2, 32), (3, 16)), jnp.float32),
        "east_courant": jnp.clip(jax.random.uniform(key_list[1], (LEV, NLAT, NLON), jnp.float32, -0.45, 0.45) * shard_levels(key_list[1], (LEV, NLAT, NLON), ((1, 32), (2, 16)), -0.4, 0.0), -0.45, 0.45),
        "north_courant": jnp.clip(jax.random.uniform(key_list[2], (LEV, NLAT, NLON), jnp.float32, -0.45, 0.45) * shard_levels(key_list[2], (LEV, NLAT, NLON), ((1, 32), (2, 16)), -0.4, 0.0), -0.45, 0.45),
        "offsets": touch_ends(jax.random.randint(key_list[3], (NLAT,), 0 - N_LON // 2, N_LON // 2), jax.random.fold_in(key_list[3], 1), 0 - N_LON // 2, (N_LON // 2) - 1).astype(jnp.int32),
        "lower_blocks": gaussian(key_list[4], (NF, NF, LEV - 1, NLAT), 0.1, 0.4, ((3, 32),), jnp.float32),
        "pivot_inverse": draw_pivot_inverse(jax.random.fold_in(key_list[7], 71), 0),
        "upper_blocks": gaussian(key_list[6], (NF, NF, LEV - 1, NLAT), 0.1, 0.4, ((3, 32),), jnp.float32),
    }


def shift_field(field, offsets):
    columns = jnp.arange(NLON, dtype=jnp.int32)
    source = jnp.mod(columns[None, :] - offsets[:, None].astype(jnp.int32) * LON_DEV, NLON).astype(jnp.int32)
    return jnp.take_along_axis(field, jnp.broadcast_to(source[None], field.shape), axis=-1)


def advect(moved, east_courant, north_wall):
    east = jnp.roll(moved, -1, axis=-1)
    east_flux = jnp.maximum(east_courant, 0.0) * moved + jnp.minimum(east_courant, 0.0) * east
    west_flux = jnp.roll(east_flux, 1, axis=-1)
    zero_row = jnp.zeros_like(moved[:, :1, :])
    north = jnp.concatenate([moved[:, 1:, :], zero_row], axis=1)
    north_flux = jnp.maximum(north_wall, 0.0) * moved + jnp.minimum(north_wall, 0.0) * north
    south_flux = jnp.concatenate([zero_row, north_flux[:, :-1, :]], axis=1)
    return moved - (east_flux - west_flux) - (north_flux - south_flux)


def apply_block(block, vector):
    return jnp.einsum("abj,bji->aji", block, vector, precision=lax.Precision.HIGHEST)


def column_solve(advected, lower_blocks, pivot_inverse, upper_blocks):
    first = apply_block(pivot_inverse[:, :, 0], advected[:, 0])

    def forward_step(previous, inputs):
        right, lower, pivot = inputs
        current = apply_block(pivot, right - apply_block(lower, previous))
        return current, current

    inputs = (jnp.moveaxis(advected[:, 1:], 1, 0), jnp.moveaxis(lower_blocks, 2, 0), jnp.moveaxis(pivot_inverse[:, :, 1:], 2, 0))
    last, rest = lax.scan(forward_step, first, inputs)
    forward = jnp.concatenate([first[None], rest], axis=0)

    def backward_step(following, inputs):
        current_forward, upper = inputs
        current = current_forward - apply_block(upper, following)
        return current, current

    top, lower_rest = lax.scan(backward_step, last, (forward[:-1], jnp.moveaxis(upper_blocks, 2, 0)), reverse=True)
    solved = jnp.concatenate([lower_rest, last[None]], axis=0)
    return jnp.moveaxis(solved, 0, 1)


def reference(fields, east_courant, north_courant, offsets, lower_blocks, pivot_inverse, upper_blocks):
    rows = jnp.arange(NLAT, dtype=jnp.int32)
    north_wall = jnp.where((rows == NLAT - 1)[None, :, None], 0.0, north_courant)

    def one_field(field):
        return advect(shift_field(field, offsets), east_courant, north_wall)

    advected = lax.map(one_field, fields)
    return column_solve(advected, lower_blocks, pivot_inverse, upper_blocks)
```

```python
import jax
import jax.numpy as jnp
from jax import lax
from jax.sharding import PartitionSpec as P


def padded(block, sides, width, periodic):
    for axis, dim in sides:
        count = lax.axis_size(axis)
        forward = [(i, i + 1) for i in range(count - 1)]
        if periodic:
            forward.append((count - 1, 0))
        backward = [(target, source) for source, target in forward]
        low = lax.ppermute(
            lax.slice_in_dim(block, block.shape[dim] - width, None, axis=dim), axis, forward
        )
        high = lax.ppermute(lax.slice_in_dim(block, 0, width, axis=dim), axis, backward)
        block = jnp.concatenate([low, block, high], axis=dim)
    return block


def apply_block(block, vector):
    return jnp.einsum("abj,bji->aji", block, vector, precision=lax.Precision.HIGHEST)


def column_solve(advected, lower_blocks, pivot_inverse, upper_blocks):
    first = apply_block(pivot_inverse[:, :, 0], advected[:, 0])

    def forward_step(previous, inputs):
        right, lower, pivot = inputs
        current = apply_block(pivot, right - apply_block(lower, previous))
        return (current, current)

    inputs = (
        jnp.moveaxis(advected[:, 1:], 1, 0),
        jnp.moveaxis(lower_blocks, 2, 0),
        jnp.moveaxis(pivot_inverse[:, :, 1:], 2, 0),
    )
    last, rest = lax.scan(forward_step, first, inputs)
    forward = jnp.concatenate([first[None], rest], axis=0)

    def backward_step(following, inputs):
        current_forward, upper = inputs
        current = current_forward - apply_block(upper, following)
        return (current, current)

    top, lower_rest = lax.scan(
        backward_step, last, (forward[:-1], jnp.moveaxis(upper_blocks, 2, 0)), reverse=True
    )
    solved = jnp.concatenate([lower_rest, last[None]], axis=0)
    return jnp.moveaxis(solved, 0, 1)


def body(fields, east_courant, north_courant, offsets, lower_blocks, pivot_inverse, upper_blocks):
    cycle_count = lax.axis_size("lon")
    band_place = lax.axis_index("lat")
    row_count = fields.shape[2]
    field_count = fields.shape[0]
    displace = jnp.mod(offsets, cycle_count)

    def shift_by(step):
        pairs = [(place, (place + step) % cycle_count) for place in range(cycle_count)]

        def branch(block):
            return block if step == 0 else lax.ppermute(block, "lon", pairs)

        return branch

    moved = lax.switch(displace[0], [shift_by(step) for step in range(cycle_count)], fields)
    global_rows = band_place * row_count + jnp.arange(row_count, dtype=jnp.int32)
    total_rows = row_count * lax.axis_size("lat")
    north_wall = jnp.where((global_rows == total_rows - 1)[None, :, None], 0.0, north_courant)
    lat_stack = jnp.concatenate([moved, north_wall[None]], axis=0)
    lon_stack = jnp.concatenate([moved, east_courant[None]], axis=0)
    lat_padded = padded(lat_stack, (("lat", 2),), 1, False)
    lon_padded = padded(lon_stack, (("lon", 3),), 1, True)
    east_flux = (
        jnp.maximum(east_courant, 0.0) * moved
        + jnp.minimum(east_courant, 0.0) * lon_padded[:field_count, :, :, 2:]
    )
    west_courant = lon_padded[field_count, :, :, :-2]
    west_flux = (
        jnp.maximum(west_courant, 0.0) * lon_padded[:field_count, :, :, :-2]
        + jnp.minimum(west_courant, 0.0) * moved
    )
    north_flux = (
        jnp.maximum(north_wall, 0.0) * moved
        + jnp.minimum(north_wall, 0.0) * lat_padded[:field_count, :, 2:, :]
    )
    south_courant = lat_padded[field_count, :, :-2, :]
    south_flux = (
        jnp.maximum(south_courant, 0.0) * lat_padded[:field_count, :, :-2, :]
        + jnp.minimum(south_courant, 0.0) * moved
    )
    advected = moved - (east_flux - west_flux) - (north_flux - south_flux)
    return column_solve(advected, lower_blocks, pivot_inverse, upper_blocks)


def solution(mesh):
    in_specs = (
        P(None, None, "lat", "lon"),
        P(None, "lat", "lon"),
        P(None, "lat", "lon"),
        P("lat"),
        P(None, None, None, "lat"),
        P(None, None, None, "lat"),
        P(None, None, None, "lat"),
    )
    out_specs = P(None, None, "lat", "lon")
    return jax.shard_map(body, mesh=mesh, in_specs=in_specs, out_specs=out_specs, check_vma=False)
```

```python
import jax
import jax.numpy as jnp
from jax import lax
from jax.experimental import pallas as pl
from jax.experimental.pallas import tpu as pltpu
from jax.sharding import PartitionSpec as P

LANES = 128
SUB = 8


def pack_column(values, lane):
    spot = lax.broadcasted_iota(jnp.int32, (SUB, LANES), 1)
    packed = jnp.zeros((SUB, LANES), jnp.float32)
    for group in range(values.shape[0] // SUB):
        tile = values[group * SUB:(group + 1) * SUB]
        turn = (group - lane) % LANES
        packed = jnp.where(spot == group, pltpu.roll(tile, turn, 1) if turn else tile, packed)
    return packed


def unpack_column(packed, first, count):
    tiles = []
    for group in range(first, first + count):
        turn = (-group) % LANES
        tiles.append(pltpu.roll(packed, turn, 1) if turn else packed)
    return jnp.concatenate(tiles, axis=0)


def kernel(
    sizes, moved_ref, east_ref, north_ref, lower_ref, pivot_ref, upper_ref, out_ref,
    north_buf, south_buf, wall_buf, west_out, east_out, west_buf, east_buf, inverse, advected,
    send_sem, recv_sem,
):
    count, levels, lat_count, lon_count = sizes
    rows = count * levels
    groups = rows // SUB
    lat, lon = lax.axis_index("lat"), lax.axis_index("lon")
    north, south = lax.rem(lat + 1, lat_count), lax.rem(lat + lat_count - 1, lat_count)
    east, west = lax.rem(lon + 1, lon_count), lax.rem(lon + lon_count - 1, lon_count)
    barrier = pltpu.get_barrier_semaphore()
    for device in ({"lat": north}, {"lat": south}, {"lon": east}, {"lon": west}):
        pl.semaphore_signal(barrier, inc=1, device_id=device, device_id_type=pl.DeviceIdType.MESH)

    own = [moved_ref[pl.ds(half, rows, stride=2), :] for half in range(2)]
    courant = [east_ref[pl.ds(half, levels, stride=2), :] for half in range(2)]
    west_out[...] = pack_column(jnp.concatenate([own[1], courant[1]], axis=0), LANES - 1)
    east_out[...] = pack_column(own[0], 0)
    pl.semaphore_wait(barrier, 4)

    def send(source, target, slot, device):
        copy = pltpu.make_async_remote_copy(
            src_ref=source, dst_ref=target, send_sem=send_sem.at[slot], recv_sem=recv_sem.at[slot],
            device_id=device, device_id_type=pl.DeviceIdType.MESH,
        )
        copy.start()
        return copy

    copies = [
        send(moved_ref, north_buf, 0, {"lat": south}),
        send(moved_ref, south_buf, 1, {"lat": north}),
        send(north_ref, wall_buf, 2, {"lat": north}),
        send(west_out, west_buf, 3, {"lon": east}),
        send(east_out, east_buf, 4, {"lon": west}),
    ]

    width = inverse.shape[1]
    place = lax.broadcasted_iota(jnp.int32, (1, width), 1)
    advected[rows:, :] = jnp.zeros((width - rows, 2 * LANES), jnp.float32)

    def product(block_ref, level, vectors):
        result = []
        for a in range(count):
            total = block_ref[a * count, level] * vectors[0]
            for b in range(1, count):
                total = total + block_ref[a * count + b, level] * vectors[b]
            result.append(total)
        return result

    def unit(level):
        return [jnp.where(place == b * levels + level, 1.0, 0.0).astype(jnp.float32) for b in range(count)]

    def keep(level, vectors):
        for a in range(count):
            inverse[pl.ds(a * levels + level, 1), :] = vectors[a]

    first = product(pivot_ref, 0, unit(0))
    keep(0, first)

    def forward_step(level, previous):
        coupled = product(lower_ref, level - 1, previous)
        right = [one - other for one, other in zip(unit(level), coupled)]
        current = product(pivot_ref, level, right)
        keep(level, current)
        return tuple(current)

    last = lax.fori_loop(1, levels, forward_step, tuple(first))

    def backward_step(step, following):
        level = levels - 2 - step
        coupled = product(upper_ref, level, following)
        current = [inverse[pl.ds(a * levels + level, 1), :] - coupled[a] for a in range(count)]
        keep(level, current)
        return tuple(current)

    lax.fori_loop(0, levels - 1, backward_step, last)

    for copy in copies:
        copy.wait()

    spot = lax.broadcasted_iota(jnp.int32, (rows, LANES), 1)
    shape = (count, levels, LANES)

    def upwind(speed, behind, ahead):
        return (
            jnp.maximum(speed, 0.0)[None] * behind.reshape(shape)
            + jnp.minimum(speed, 0.0)[None] * ahead.reshape(shape)
        ).reshape(rows, LANES)

    east_edge = unpack_column(east_buf[...], 0, groups)
    west_edge = unpack_column(west_buf[...], 0, groups)
    west_speed = unpack_column(west_buf[...], groups, levels // SUB)
    flux = [
        upwind(courant[0], own[0], pltpu.roll(jnp.where(spot == 0, own[1], own[0]), LANES - 1, 1)),
        upwind(courant[1], own[1], pltpu.roll(jnp.where(spot == 0, east_edge, own[1]), LANES - 1, 1)),
    ]
    from_west = [
        jnp.where(spot == 0, upwind(west_speed, west_edge, own[0]), pltpu.roll(flux[0], 1, 1)),
        pltpu.roll(jnp.where(spot == LANES - 1, flux[0], flux[1]), 1, 1),
    ]
    for half in range(2):
        part, level_part = pl.ds(half, rows, stride=2), pl.ds(half, levels, stride=2)
        north_wall = jnp.where(lat == lat_count - 1, 0.0, north_ref[level_part, :])
        south_wall = jnp.where(lat == 0, 0.0, wall_buf[level_part, :])
        to_north = upwind(north_wall, own[half], north_buf[part, :])
        from_south = upwind(south_wall, south_buf[part, :], own[half])
        advected[:rows, half * LANES:(half + 1) * LANES] = (
            own[half] - (flux[half] - from_west[half]) - (to_north - from_south)
        )
    solved = lax.dot_general(
        inverse[...], advected[...], (((1,), (0,)), ((), ())),
        precision=lax.Precision.HIGHEST, preferred_element_type=jnp.float32,
    )
    for half in range(2):
        out_ref[pl.ds(half, rows, stride=2), :] = solved[:, half * LANES:(half + 1) * LANES]


def body(fields, east_courant, north_courant, offsets, lower_blocks, pivot_inverse, upper_blocks):
    cycle_count = lax.axis_size("lon")
    band_count = lax.axis_size("lat")
    count, levels = fields.shape[:2]
    rows = count * levels
    displace = jnp.mod(offsets, cycle_count)

    def shift_by(step):
        pairs = [(place, (place + step) % cycle_count) for place in range(cycle_count)]

        def branch(block):
            return block if step == 0 else lax.ppermute(block, "lon", pairs)

        return branch

    moved = lax.switch(
        displace[0], [shift_by(step) for step in range(cycle_count)], fields.reshape(2 * rows, LANES)
    )
    width = -(-rows // 256) * 256
    vmem = pl.BlockSpec(memory_space=pltpu.VMEM)
    smem = pl.BlockSpec(memory_space=pltpu.SMEM)
    solved = pl.pallas_call(
        lambda *refs: kernel((count, levels, band_count, cycle_count), *refs),
        out_shape=jax.ShapeDtypeStruct((2 * rows, LANES), jnp.float32),
        in_specs=[vmem] * 3 + [smem] * 3,
        out_specs=vmem,
        scratch_shapes=[
            pltpu.VMEM((2 * rows, LANES), jnp.float32),
            pltpu.VMEM((2 * rows, LANES), jnp.float32),
            pltpu.VMEM((2 * levels, LANES), jnp.float32),
            pltpu.VMEM((SUB, LANES), jnp.float32),
            pltpu.VMEM((SUB, LANES), jnp.float32),
            pltpu.VMEM((SUB, LANES), jnp.float32),
            pltpu.VMEM((SUB, LANES), jnp.float32),
            pltpu.VMEM((rows, width), jnp.float32),
            pltpu.VMEM((width, 2 * LANES), jnp.float32),
            pltpu.SemaphoreType.DMA((5,)),
            pltpu.SemaphoreType.DMA((5,)),
        ],
        compiler_params=pltpu.CompilerParams(collective_id=0, has_side_effects=True),
    )(
        moved,
        east_courant.reshape(2 * levels, LANES),
        north_courant.reshape(2 * levels, LANES),
        lower_blocks.reshape(count * count, levels - 1),
        pivot_inverse.reshape(count * count, levels),
        upper_blocks.reshape(count * count, levels - 1),
    )
    return solved.reshape(fields.shape)


def solution(mesh):
    in_specs = (
        P(None, None, "lat", "lon"),
        P(None, "lat", "lon"),
        P(None, "lat", "lon"),
        P("lat"),
        P(None, None, None, "lat"),
        P(None, None, None, "lat"),
        P(None, None, None, "lat"),
    )
    out_specs = P(None, None, "lat", "lon")
    return jax.shard_map(body, mesh=mesh, in_specs=in_specs, out_specs=out_specs, check_vma=False)
```

```python
import jax
import jax.numpy as jnp
from jax import lax
from jax.experimental import pallas as pl
from jax.experimental.pallas import tpu as pltpu
from jax.sharding import PartitionSpec as P

LANES = 128
SUB = 8


def pack_column(values, lane):
    spot = lax.broadcasted_iota(jnp.int32, (SUB, LANES), 1)
    packed = jnp.zeros((SUB, LANES), jnp.float32)
    for group in range(values.shape[0] // SUB):
        tile = values[group * SUB:(group + 1) * SUB]
        turn = (group - lane) % LANES
        packed = jnp.where(spot == group, pltpu.roll(tile, turn, 1) if turn else tile, packed)
    return packed


def unpack_column(packed, first, count):
    tiles = []
    for group in range(first, first + count):
        turn = (-group) % LANES
        tiles.append(pltpu.roll(packed, turn, 1) if turn else packed)
    return jnp.concatenate(tiles, axis=0)


def kernel(
    sizes, moved_ref, east_ref, north_ref, lower_ref, pivot_ref, upper_ref, inverse, advected,
    north_buf, south_buf, wall_buf, west_out, east_out, west_buf, east_buf, base,
    send_sem, recv_sem,
):
    count, levels, lat_count, lon_count = sizes
    rows = count * levels
    groups = rows // SUB
    lat, lon = lax.axis_index("lat"), lax.axis_index("lon")
    north, south = lax.rem(lat + 1, lat_count), lax.rem(lat + lat_count - 1, lat_count)
    east, west = lax.rem(lon + 1, lon_count), lax.rem(lon + lon_count - 1, lon_count)
    barrier = pltpu.get_barrier_semaphore()
    for device in ({"lat": north}, {"lat": south}, {"lon": east}, {"lon": west}):
        pl.semaphore_signal(barrier, inc=1, device_id=device, device_id_type=pl.DeviceIdType.MESH)

    own = [moved_ref[pl.ds(half, rows, stride=2), :] for half in range(2)]
    courant = [east_ref[pl.ds(half, levels, stride=2), :] for half in range(2)]
    west_out[...] = pack_column(jnp.concatenate([own[1], courant[1]], axis=0), LANES - 1)
    east_out[...] = pack_column(own[0], 0)
    pl.semaphore_wait(barrier, 4)

    def send(source, target, slot, device):
        copy = pltpu.make_async_remote_copy(
            src_ref=source, dst_ref=target, send_sem=send_sem.at[slot], recv_sem=recv_sem.at[slot],
            device_id=device, device_id_type=pl.DeviceIdType.MESH,
        )
        copy.start()
        return copy

    copies = [
        send(moved_ref, north_buf, 0, {"lat": south}),
        send(moved_ref, south_buf, 1, {"lat": north}),
        send(north_ref, wall_buf, 2, {"lat": north}),
        send(west_out, west_buf, 3, {"lon": east}),
        send(east_out, east_buf, 4, {"lon": west}),
    ]

    width = inverse.shape[1]
    place = lax.broadcasted_iota(jnp.int32, (1, width), 1)
    advected[rows:, :] = jnp.zeros((width - rows, 2 * LANES), jnp.float32)

    def product(block_ref, level, vectors):
        result = []
        for a in range(count):
            total = block_ref[a * count, 0, level] * vectors[0]
            for b in range(1, count):
                total = total + block_ref[a * count + b, 0, level] * vectors[b]
            result.append(total)
        return result

    def unit(level):
        return [jnp.where(place == b * levels + level, 1.0, 0.0).astype(jnp.float32) for b in range(count)]

    def keep(level, vectors):
        for a in range(count):
            inverse[pl.ds(a * levels + level, 1), :] = vectors[a]

    first = product(pivot_ref, 0, unit(0))
    keep(0, first)

    def forward_step(level, previous):
        coupled = product(lower_ref, level - 1, previous)
        right = [one - other for one, other in zip(unit(level), coupled)]
        current = product(pivot_ref, level, right)
        keep(level, current)
        return tuple(current)

    last = lax.fori_loop(1, levels, forward_step, tuple(first))

    def backward_step(step, following):
        level = levels - 2 - step
        coupled = product(upper_ref, level, following)
        current = [inverse[pl.ds(a * levels + level, 1), :] - coupled[a] for a in range(count)]
        keep(level, current)
        return tuple(current)

    lax.fori_loop(0, levels - 1, backward_step, last)

    for copy in copies[2:]:
        copy.wait()

    spot = lax.broadcasted_iota(jnp.int32, (rows, LANES), 1)
    shape = (count, levels, LANES)

    def upwind(speed, behind, ahead):
        return (
            jnp.maximum(speed, 0.0)[None] * behind.reshape(shape)
            + jnp.minimum(speed, 0.0)[None] * ahead.reshape(shape)
        ).reshape(rows, LANES)

    east_edge = unpack_column(east_buf[...], 0, groups)
    west_edge = unpack_column(west_buf[...], 0, groups)
    west_speed = unpack_column(west_buf[...], groups, levels // SUB)
    flux = [
        upwind(courant[0], own[0], pltpu.roll(jnp.where(spot == 0, own[1], own[0]), LANES - 1, 1)),
        upwind(courant[1], own[1], pltpu.roll(jnp.where(spot == 0, east_edge, own[1]), LANES - 1, 1)),
    ]
    from_west = [
        jnp.where(spot == 0, upwind(west_speed, west_edge, own[0]), pltpu.roll(flux[0], 1, 1)),
        pltpu.roll(jnp.where(spot == LANES - 1, flux[0], flux[1]), 1, 1),
    ]
    for half in range(2):
        base[half] = own[half] - (flux[half] - from_west[half])
    for copy in copies[:2]:
        copy.wait()
    for half in range(2):
        part, level_part = pl.ds(half, rows, stride=2), pl.ds(half, levels, stride=2)
        north_wall = jnp.where(lat == lat_count - 1, 0.0, north_ref[level_part, :])
        south_wall = jnp.where(lat == 0, 0.0, wall_buf[level_part, :])
        middle = moved_ref[part, :]
        to_north = upwind(north_wall, middle, north_buf[part, :])
        from_south = upwind(south_wall, south_buf[part, :], middle)
        advected[:rows, half * LANES:(half + 1) * LANES] = base[half] - (to_north - from_south)


def apply_inverse(inverse, advected, out_ref):
    solved = lax.dot_general(
        inverse[...], advected[...], (((1,), (0,)), ((), ())),
        precision=lax.Precision.HIGHEST, preferred_element_type=jnp.float32,
    )
    for half in range(2):
        out_ref[pl.ds(half, inverse.shape[0], stride=2), :] = solved[:, half * LANES:(half + 1) * LANES]


def body(fields, east_courant, north_courant, offsets, lower_blocks, pivot_inverse, upper_blocks):
    cycle_count = lax.axis_size("lon")
    band_count = lax.axis_size("lat")
    count, levels = fields.shape[:2]
    rows = count * levels
    displace = jnp.mod(offsets, cycle_count)

    def shift_by(step):
        pairs = [(place, (place + step) % cycle_count) for place in range(cycle_count)]

        def branch(block):
            return block if step == 0 else lax.ppermute(block, "lon", pairs)

        return branch

    moved = lax.switch(
        displace[0], [shift_by(step) for step in range(cycle_count)], fields.reshape(2 * rows, LANES)
    )
    width = -(-rows // 256) * 256
    vmem = pl.BlockSpec(memory_space=pltpu.VMEM)
    smem = pl.BlockSpec(memory_space=pltpu.SMEM)
    inverse, advected = pl.pallas_call(
        lambda *refs: kernel((count, levels, band_count, cycle_count), *refs),
        out_shape=(
            jax.ShapeDtypeStruct((rows, width), jnp.float32),
            jax.ShapeDtypeStruct((width, 2 * LANES), jnp.float32),
        ),
        in_specs=[vmem] * 3 + [smem] * 3,
        out_specs=(vmem, vmem),
        scratch_shapes=[
            pltpu.VMEM((2 * rows, LANES), jnp.float32),
            pltpu.VMEM((2 * rows, LANES), jnp.float32),
            pltpu.VMEM((2 * levels, LANES), jnp.float32),
            pltpu.VMEM((SUB, LANES), jnp.float32),
            pltpu.VMEM((SUB, LANES), jnp.float32),
            pltpu.VMEM((SUB, LANES), jnp.float32),
            pltpu.VMEM((SUB, LANES), jnp.float32),
            pltpu.VMEM((2, rows, LANES), jnp.float32),
            pltpu.SemaphoreType.DMA((5,)),
            pltpu.SemaphoreType.DMA((5,)),
        ],
        compiler_params=pltpu.CompilerParams(
            collective_id=0, has_side_effects=True, vmem_limit_bytes=8 * 1024 * 1024
        ),
    )(
        moved,
        east_courant.reshape(2 * levels, LANES),
        north_courant.reshape(2 * levels, LANES),
        jnp.swapaxes(lower_blocks, 2, 3).reshape(count * count, 1, levels - 1),
        jnp.swapaxes(pivot_inverse, 2, 3).reshape(count * count, 1, levels),
        jnp.swapaxes(upper_blocks, 2, 3).reshape(count * count, 1, levels - 1),
    )
    solved = pl.pallas_call(
        apply_inverse,
        out_shape=jax.ShapeDtypeStruct((2 * rows, LANES), jnp.float32),
        in_specs=[vmem] * 2,
        out_specs=vmem,
        compiler_params=pltpu.CompilerParams(vmem_limit_bytes=8 * 1024 * 1024),
    )(inverse, advected)
    return solved.reshape(fields.shape)


def solution(mesh):
    in_specs = (
        P(None, None, "lat", "lon"),
        P(None, "lat", "lon"),
        P(None, "lat", "lon"),
        P("lat"),
        P(None, None, None, "lat"),
        P(None, None, None, "lat"),
        P(None, None, None, "lat"),
    )
    out_specs = P(None, None, "lat", "lon")
    return jax.shard_map(body, mesh=mesh, in_specs=in_specs, out_specs=out_specs, check_vma=False)
```

```python
import jax
import jax.numpy as jnp
from jax import lax
from jax.experimental import pallas as pl
from jax.experimental.pallas import tpu as pltpu
from jax.sharding import PartitionSpec as P

LANES = 128
SUB = 8


def pack_column(values, lane):
    spot = lax.broadcasted_iota(jnp.int32, (SUB, LANES), 1)
    packed = jnp.zeros((SUB, LANES), jnp.float32)
    for group in range(values.shape[0] // SUB):
        tile = values[group * SUB:(group + 1) * SUB]
        turn = (group - lane) % LANES
        packed = jnp.where(spot == group, pltpu.roll(tile, turn, 1) if turn else tile, packed)
    return packed


def unpack_column(packed, first, count):
    tiles = []
    for group in range(first, first + count):
        turn = (-group) % LANES
        tiles.append(pltpu.roll(packed, turn, 1) if turn else packed)
    return jnp.concatenate(tiles, axis=0)


def kernel(
    sizes, moved_ref, east_ref, north_ref, lower_ref, pivot_ref, upper_ref, inverse, advected,
    lat_buf, wall_buf, west_out, east_out, west_buf, east_buf, base,
    send_sem, recv_sem,
):
    count, levels, lat_count, lon_count = sizes
    rows = count * levels
    groups = rows // SUB
    lat, lon = lax.axis_index("lat"), lax.axis_index("lon")
    north, south = lax.rem(lat + 1, lat_count), lax.rem(lat + lat_count - 1, lat_count)
    east, west = lax.rem(lon + 1, lon_count), lax.rem(lon + lon_count - 1, lon_count)
    barrier = pltpu.get_barrier_semaphore()
    for device in ({"lat": north}, {"lat": south}, {"lon": east}, {"lon": west}):
        pl.semaphore_signal(barrier, inc=1, device_id=device, device_id_type=pl.DeviceIdType.MESH)

    own = [moved_ref[pl.ds(half, rows, stride=2), :] for half in range(2)]
    courant = [east_ref[pl.ds(half, levels, stride=2), :] for half in range(2)]
    west_out[...] = pack_column(jnp.concatenate([own[1], courant[1]], axis=0), LANES - 1)
    east_out[...] = pack_column(own[0], 0)
    pl.semaphore_wait(barrier, 4)

    def send(source, target, slot, device):
        copy = pltpu.make_async_remote_copy(
            src_ref=source, dst_ref=target, send_sem=send_sem.at[slot], recv_sem=recv_sem.at[slot],
            device_id=device, device_id_type=pl.DeviceIdType.MESH,
        )
        copy.start()
        return copy

    far = lax.rem(lat, 2)
    near = 1 - far
    copies = [
        send(west_out, west_buf, 3, {"lon": east}),
        send(east_out, east_buf, 4, {"lon": west}),
        send(moved_ref, lat_buf.at[far], far, {"lat": jnp.where(far == 1, north, south)}),
        send(north_ref, wall_buf, 2, {"lat": north}),
        send(moved_ref, lat_buf.at[near], near, {"lat": jnp.where(far == 1, south, north)}),
    ]

    width = inverse.shape[1]
    place = lax.broadcasted_iota(jnp.int32, (1, width), 1)
    advected[rows:, :] = jnp.zeros((width - rows, 2 * LANES), jnp.float32)

    def product(block_ref, level, vectors):
        result = []
        for a in range(count):
            total = block_ref[a * count, 0, level] * vectors[0]
            for b in range(1, count):
                total = total + block_ref[a * count + b, 0, level] * vectors[b]
            result.append(total)
        return result

    def unit(level):
        return [jnp.where(place == b * levels + level, 1.0, 0.0).astype(jnp.float32) for b in range(count)]

    def keep(level, vectors):
        for a in range(count):
            inverse[pl.ds(a * levels + level, 1), :] = vectors[a]

    first = product(pivot_ref, 0, unit(0))
    keep(0, first)

    def forward_step(level, previous):
        coupled = product(lower_ref, level - 1, previous)
        right = [one - other for one, other in zip(unit(level), coupled)]
        current = product(pivot_ref, level, right)
        keep(level, current)
        return tuple(current)

    last = lax.fori_loop(1, levels, forward_step, tuple(first))

    def backward_step(step, following):
        level = levels - 2 - step
        coupled = product(upper_ref, level, following)
        current = [inverse[pl.ds(a * levels + level, 1), :] - coupled[a] for a in range(count)]
        keep(level, current)
        return tuple(current)

    lax.fori_loop(0, levels - 1, backward_step, last)

    for copy in copies[:2]:
        copy.wait()

    spot = lax.broadcasted_iota(jnp.int32, (rows, LANES), 1)
    shape = (count, levels, LANES)

    def upwind(speed, behind, ahead):
        return (
            jnp.maximum(speed, 0.0)[None] * behind.reshape(shape)
            + jnp.minimum(speed, 0.0)[None] * ahead.reshape(shape)
        ).reshape(rows, LANES)

    east_edge = unpack_column(east_buf[...], 0, groups)
    west_edge = unpack_column(west_buf[...], 0, groups)
    west_speed = unpack_column(west_buf[...], groups, levels // SUB)
    flux = [
        upwind(courant[0], own[0], pltpu.roll(jnp.where(spot == 0, own[1], own[0]), LANES - 1, 1)),
        upwind(courant[1], own[1], pltpu.roll(jnp.where(spot == 0, east_edge, own[1]), LANES - 1, 1)),
    ]
    from_west = [
        jnp.where(spot == 0, upwind(west_speed, west_edge, own[0]), pltpu.roll(flux[0], 1, 1)),
        pltpu.roll(jnp.where(spot == LANES - 1, flux[0], flux[1]), 1, 1),
    ]
    for half in range(2):
        base[half] = own[half] - (flux[half] - from_west[half])
    for copy in copies[2:]:
        copy.wait()
    for half in range(2):
        part, level_part = pl.ds(half, rows, stride=2), pl.ds(half, levels, stride=2)
        north_wall = jnp.where(lat == lat_count - 1, 0.0, north_ref[level_part, :])
        south_wall = jnp.where(lat == 0, 0.0, wall_buf[level_part, :])
        middle = moved_ref[part, :]
        to_north = upwind(north_wall, middle, lat_buf[0, part, :])
        from_south = upwind(south_wall, lat_buf[1, part, :], middle)
        advected[:rows, half * LANES:(half + 1) * LANES] = base[half] - (to_north - from_south)


def apply_inverse(inverse, advected, out_ref):
    solved = lax.dot_general(
        inverse[...], advected[...], (((1,), (0,)), ((), ())),
        precision=lax.Precision.HIGHEST, preferred_element_type=jnp.float32,
    )
    for half in range(2):
        out_ref[pl.ds(half, inverse.shape[0], stride=2), :] = solved[:, half * LANES:(half + 1) * LANES]


def body(fields, east_courant, north_courant, offsets, lower_blocks, pivot_inverse, upper_blocks):
    cycle_count = lax.axis_size("lon")
    band_count = lax.axis_size("lat")
    count, levels = fields.shape[:2]
    rows = count * levels
    displace = jnp.mod(offsets, cycle_count)

    def shift_by(step):
        pairs = [(place, (place + step) % cycle_count) for place in range(cycle_count)]

        def branch(block):
            return block if step == 0 else lax.ppermute(block, "lon", pairs)

        return branch

    moved = lax.switch(
        displace[0], [shift_by(step) for step in range(cycle_count)], fields.reshape(2 * rows, LANES)
    )
    width = -(-rows // 256) * 256
    vmem = pl.BlockSpec(memory_space=pltpu.VMEM)
    smem = pl.BlockSpec(memory_space=pltpu.SMEM)
    inverse, advected = pl.pallas_call(
        lambda *refs: kernel((count, levels, band_count, cycle_count), *refs),
        out_shape=(
            jax.ShapeDtypeStruct((rows, width), jnp.float32),
            jax.ShapeDtypeStruct((width, 2 * LANES), jnp.float32),
        ),
        in_specs=[vmem] * 3 + [smem] * 3,
        out_specs=(vmem, vmem),
        scratch_shapes=[
            pltpu.VMEM((2, 2 * rows, LANES), jnp.float32),
            pltpu.VMEM((2 * levels, LANES), jnp.float32),
            pltpu.VMEM((SUB, LANES), jnp.float32),
            pltpu.VMEM((SUB, LANES), jnp.float32),
            pltpu.VMEM((SUB, LANES), jnp.float32),
            pltpu.VMEM((SUB, LANES), jnp.float32),
            pltpu.VMEM((2, rows, LANES), jnp.float32),
            pltpu.SemaphoreType.DMA((5,)),
            pltpu.SemaphoreType.DMA((5,)),
        ],
        compiler_params=pltpu.CompilerParams(
            collective_id=0, has_side_effects=True, vmem_limit_bytes=8 * 1024 * 1024
        ),
    )(
        moved,
        east_courant.reshape(2 * levels, LANES),
        north_courant.reshape(2 * levels, LANES),
        jnp.swapaxes(lower_blocks, 2, 3).reshape(count * count, 1, levels - 1),
        jnp.swapaxes(pivot_inverse, 2, 3).reshape(count * count, 1, levels),
        jnp.swapaxes(upper_blocks, 2, 3).reshape(count * count, 1, levels - 1),
    )
    solved = pl.pallas_call(
        apply_inverse,
        out_shape=jax.ShapeDtypeStruct((2 * rows, LANES), jnp.float32),
        in_specs=[vmem] * 2,
        out_specs=vmem,
        compiler_params=pltpu.CompilerParams(vmem_limit_bytes=8 * 1024 * 1024),
    )(inverse, advected)
    return solved.reshape(fields.shape)


def solution(mesh):
    in_specs = (
        P(None, None, "lat", "lon"),
        P(None, "lat", "lon"),
        P(None, "lat", "lon"),
        P("lat"),
        P(None, None, None, "lat"),
        P(None, None, None, "lat"),
        P(None, None, None, "lat"),
    )
    out_specs = P(None, None, "lat", "lon")
    return jax.shard_map(body, mesh=mesh, in_specs=in_specs, out_specs=out_specs, check_vma=False)
```

```python
import jax
import jax.numpy as jnp
from jax import lax
from jax.experimental import pallas as pl
from jax.experimental.pallas import tpu as pltpu
from jax.sharding import PartitionSpec as P

LANES = 128
SUB = 8


def pack_column(values, lane):
    spot = lax.broadcasted_iota(jnp.int32, (SUB, LANES), 1)
    packed = jnp.zeros((SUB, LANES), jnp.float32)
    for group in range(values.shape[0] // SUB):
        tile = values[group * SUB:(group + 1) * SUB]
        turn = (group - lane) % LANES
        packed = jnp.where(spot == group, pltpu.roll(tile, turn, 1) if turn else tile, packed)
    return packed


def unpack_column(packed, first, count):
    tiles = []
    for group in range(first, first + count):
        turn = (-group) % LANES
        tiles.append(pltpu.roll(packed, turn, 1) if turn else packed)
    return jnp.concatenate(tiles, axis=0)


def kernel(
    sizes, moved_ref, east_ref, north_ref, lower_ref, pivot_ref, upper_ref, inverse, advected,
    north_buf, south_buf, wall_buf, west_out, east_out, west_buf, east_buf, base,
    send_sem, recv_sem,
):
    count, levels, lat_count, lon_count = sizes
    rows = count * levels
    groups = rows // SUB
    lat, lon = lax.axis_index("lat"), lax.axis_index("lon")
    north, south = lax.rem(lat + 1, lat_count), lax.rem(lat + lat_count - 1, lat_count)
    east, west = lax.rem(lon + 1, lon_count), lax.rem(lon + lon_count - 1, lon_count)
    barrier = pltpu.get_barrier_semaphore()
    inside_north, inside_south = lat < lat_count - 1, lat > 0

    def greet(device):
        pl.semaphore_signal(barrier, inc=1, device_id=device, device_id_type=pl.DeviceIdType.MESH)

    greet({"lon": east})
    greet({"lon": west})

    @pl.when(inside_north)
    def _():
        greet({"lat": north})

    @pl.when(inside_south)
    def _():
        greet({"lat": south})


    own = [moved_ref[pl.ds(half, rows, stride=2), :] for half in range(2)]
    courant = [east_ref[pl.ds(half, levels, stride=2), :] for half in range(2)]
    west_out[...] = pack_column(jnp.concatenate([own[1], courant[1]], axis=0), LANES - 1)
    east_out[...] = pack_column(own[0], 0)
    interior = jnp.logical_and(inside_north, inside_south)

    @pl.when(interior)
    def _():
        pl.semaphore_wait(barrier, 4)

    @pl.when(jnp.logical_not(interior))
    def _():
        pl.semaphore_wait(barrier, 3)


    def link(source, target, slot, device):
        return pltpu.make_async_remote_copy(
            src_ref=source, dst_ref=target, send_sem=send_sem.at[slot], recv_sem=recv_sem.at[slot],
            device_id=device, device_id_type=pl.DeviceIdType.MESH,
        )

    to_south = link(moved_ref, north_buf, 0, {"lat": south})
    to_north_row = link(moved_ref, south_buf, 1, {"lat": north})
    wall = link(north_ref, wall_buf, 2, {"lat": north})
    edges = [link(west_out, west_buf, 3, {"lon": east}), link(east_out, east_buf, 4, {"lon": west})]
    for copy in edges:
        copy.start()

    @pl.when(inside_south)
    def _():
        to_south.start()

    @pl.when(inside_north)
    def _():
        to_north_row.start()
        wall.start()

    @pl.when(jnp.logical_not(inside_north))
    def _():
        north_buf[...] = jnp.zeros_like(north_buf)

    @pl.when(jnp.logical_not(inside_south))
    def _():
        south_buf[...] = jnp.zeros_like(south_buf)
        wall_buf[...] = jnp.zeros_like(wall_buf)

    width = inverse.shape[1]
    place = lax.broadcasted_iota(jnp.int32, (1, width), 1)
    advected[rows:, :] = jnp.zeros((width - rows, 2 * LANES), jnp.float32)

    def product(block_ref, level, vectors):
        result = []
        for a in range(count):
            total = block_ref[a * count, 0, level] * vectors[0]
            for b in range(1, count):
                total = total + block_ref[a * count + b, 0, level] * vectors[b]
            result.append(total)
        return result

    def unit(level):
        return [jnp.where(place == b * levels + level, 1.0, 0.0).astype(jnp.float32) for b in range(count)]

    def keep(level, vectors):
        for a in range(count):
            inverse[pl.ds(a * levels + level, 1), :] = vectors[a]

    first = product(pivot_ref, 0, unit(0))
    keep(0, first)

    def forward_step(level, previous):
        coupled = product(lower_ref, level - 1, previous)
        right = [one - other for one, other in zip(unit(level), coupled)]
        current = product(pivot_ref, level, right)
        keep(level, current)
        return tuple(current)

    last = lax.fori_loop(1, levels, forward_step, tuple(first))

    def backward_step(step, following):
        level = levels - 2 - step
        coupled = product(upper_ref, level, following)
        current = [inverse[pl.ds(a * levels + level, 1), :] - coupled[a] for a in range(count)]
        keep(level, current)
        return tuple(current)

    lax.fori_loop(0, levels - 1, backward_step, last)

    for copy in edges:
        copy.wait()

    spot = lax.broadcasted_iota(jnp.int32, (rows, LANES), 1)
    shape = (count, levels, LANES)

    def upwind(speed, behind, ahead):
        return (
            jnp.maximum(speed, 0.0)[None] * behind.reshape(shape)
            + jnp.minimum(speed, 0.0)[None] * ahead.reshape(shape)
        ).reshape(rows, LANES)

    east_edge = unpack_column(east_buf[...], 0, groups)
    west_edge = unpack_column(west_buf[...], 0, groups)
    west_speed = unpack_column(west_buf[...], groups, levels // SUB)
    flux = [
        upwind(courant[0], own[0], pltpu.roll(jnp.where(spot == 0, own[1], own[0]), LANES - 1, 1)),
        upwind(courant[1], own[1], pltpu.roll(jnp.where(spot == 0, east_edge, own[1]), LANES - 1, 1)),
    ]
    from_west = [
        jnp.where(spot == 0, upwind(west_speed, west_edge, own[0]), pltpu.roll(flux[0], 1, 1)),
        pltpu.roll(jnp.where(spot == LANES - 1, flux[0], flux[1]), 1, 1),
    ]
    for half in range(2):
        base[half] = own[half] - (flux[half] - from_west[half])

    @pl.when(inside_south)
    def _():
        to_south.wait_send()
        to_north_row.wait_recv()
        wall.wait_recv()

    @pl.when(inside_north)
    def _():
        to_north_row.wait_send()
        wall.wait_send()
        to_south.wait_recv()

    for half in range(2):
        part, level_part = pl.ds(half, rows, stride=2), pl.ds(half, levels, stride=2)
        north_wall = jnp.where(lat == lat_count - 1, 0.0, north_ref[level_part, :])
        south_wall = jnp.where(lat == 0, 0.0, wall_buf[level_part, :])
        middle = moved_ref[part, :]
        to_north = upwind(north_wall, middle, north_buf[part, :])
        from_south = upwind(south_wall, south_buf[part, :], middle)
        advected[:rows, half * LANES:(half + 1) * LANES] = base[half] - (to_north - from_south)


def apply_inverse(inverse, advected, out_ref):
    solved = lax.dot_general(
        inverse[...], advected[...], (((1,), (0,)), ((), ())),
        precision=lax.Precision.HIGHEST, preferred_element_type=jnp.float32,
    )
    for half in range(2):
        out_ref[pl.ds(half, inverse.shape[0], stride=2), :] = solved[:, half * LANES:(half + 1) * LANES]


def body(fields, east_courant, north_courant, offsets, lower_blocks, pivot_inverse, upper_blocks):
    cycle_count = lax.axis_size("lon")
    band_count = lax.axis_size("lat")
    count, levels = fields.shape[:2]
    rows = count * levels
    displace = jnp.mod(offsets, cycle_count)

    def shift_by(step):
        pairs = [(place, (place + step) % cycle_count) for place in range(cycle_count)]

        def branch(block):
            return block if step == 0 else lax.ppermute(block, "lon", pairs)

        return branch

    moved = lax.switch(
        displace[0], [shift_by(step) for step in range(cycle_count)], fields.reshape(2 * rows, LANES)
    )
    width = -(-rows // 256) * 256
    vmem = pl.BlockSpec(memory_space=pltpu.VMEM)
    smem = pl.BlockSpec(memory_space=pltpu.SMEM)
    inverse, advected = pl.pallas_call(
        lambda *refs: kernel((count, levels, band_count, cycle_count), *refs),
        out_shape=(
            jax.ShapeDtypeStruct((rows, width), jnp.float32),
            jax.ShapeDtypeStruct((width, 2 * LANES), jnp.float32),
        ),
        in_specs=[vmem] * 3 + [smem] * 3,
        out_specs=(vmem, vmem),
        scratch_shapes=[
            pltpu.VMEM((2 * rows, LANES), jnp.float32),
            pltpu.VMEM((2 * rows, LANES), jnp.float32),
            pltpu.VMEM((2 * levels, LANES), jnp.float32),
            pltpu.VMEM((SUB, LANES), jnp.float32),
            pltpu.VMEM((SUB, LANES), jnp.float32),
            pltpu.VMEM((SUB, LANES), jnp.float32),
            pltpu.VMEM((SUB, LANES), jnp.float32),
            pltpu.VMEM((2, rows, LANES), jnp.float32),
            pltpu.SemaphoreType.DMA((5,)),
            pltpu.SemaphoreType.DMA((5,)),
        ],
        compiler_params=pltpu.CompilerParams(
            collective_id=0, has_side_effects=True, vmem_limit_bytes=8 * 1024 * 1024
        ),
    )(
        moved,
        east_courant.reshape(2 * levels, LANES),
        north_courant.reshape(2 * levels, LANES),
        jnp.swapaxes(lower_blocks, 2, 3).reshape(count * count, 1, levels - 1),
        jnp.swapaxes(pivot_inverse, 2, 3).reshape(count * count, 1, levels),
        jnp.swapaxes(upper_blocks, 2, 3).reshape(count * count, 1, levels - 1),
    )
    solved = pl.pallas_call(
        apply_inverse,
        out_shape=jax.ShapeDtypeStruct((2 * rows, LANES), jnp.float32),
        in_specs=[vmem] * 2,
        out_specs=vmem,
        compiler_params=pltpu.CompilerParams(vmem_limit_bytes=8 * 1024 * 1024),
    )(inverse, advected)
    return solved.reshape(fields.shape)


def solution(mesh):
    in_specs = (
        P(None, None, "lat", "lon"),
        P(None, "lat", "lon"),
        P(None, "lat", "lon"),
        P("lat"),
        P(None, None, None, "lat"),
        P(None, None, None, "lat"),
        P(None, None, None, "lat"),
    )
    out_specs = P(None, None, "lat", "lon")
    return jax.shard_map(body, mesh=mesh, in_specs=in_specs, out_specs=out_specs, check_vma=False)
```

```python
import jax
import jax.numpy as jnp
from jax import lax
from jax.experimental import pallas as pl
from jax.experimental.pallas import tpu as pltpu
from jax.sharding import PartitionSpec as P

LANES = 128
SUB = 8


def pack_column(values, lane):
    spot = lax.broadcasted_iota(jnp.int32, (SUB, LANES), 1)
    packed = jnp.zeros((SUB, LANES), jnp.float32)
    for group in range(values.shape[0] // SUB):
        tile = values[group * SUB:(group + 1) * SUB]
        turn = (group - lane) % LANES
        packed = jnp.where(spot == group, pltpu.roll(tile, turn, 1) if turn else tile, packed)
    return packed


def unpack_column(packed, first, count):
    tiles = []
    for group in range(first, first + count):
        turn = (-group) % LANES
        tiles.append(pltpu.roll(packed, turn, 1) if turn else packed)
    return jnp.concatenate(tiles, axis=0)


def kernel(
    sizes, moved_ref, east_ref, north_ref, lower_ref, pivot_ref, upper_ref, inverse, advected,
    north_buf, south_buf, wall_buf, west_out, east_out, west_buf, east_buf, base,
    send_sem, recv_sem,
):
    count, levels, lat_count, lon_count = sizes
    rows = count * levels
    groups = rows // SUB
    lat, lon = lax.axis_index("lat"), lax.axis_index("lon")
    north, south = lax.rem(lat + 1, lat_count), lax.rem(lat + lat_count - 1, lat_count)
    east, west = lax.rem(lon + 1, lon_count), lax.rem(lon + lon_count - 1, lon_count)
    barrier = pltpu.get_barrier_semaphore()
    inside_north, inside_south = lat < lat_count - 1, lat > 0

    def greet(device):
        pl.semaphore_signal(barrier, inc=1, device_id=device, device_id_type=pl.DeviceIdType.MESH)

    greet({"lon": east})
    greet({"lon": west})

    @pl.when(inside_north)
    def _():
        greet({"lat": north})

    @pl.when(inside_south)
    def _():
        greet({"lat": south})


    own = [moved_ref[pl.ds(half, rows, stride=2), :] for half in range(2)]
    courant = [east_ref[pl.ds(half, levels, stride=2), :] for half in range(2)]
    west_out[...] = pack_column(jnp.concatenate([own[1], courant[1]], axis=0), LANES - 1)
    east_out[...] = pack_column(own[0], 0)
    interior = jnp.logical_and(inside_north, inside_south)

    @pl.when(interior)
    def _():
        pl.semaphore_wait(barrier, 4)

    @pl.when(jnp.logical_not(interior))
    def _():
        pl.semaphore_wait(barrier, 3)


    def link(source, target, slot, device):
        return pltpu.make_async_remote_copy(
            src_ref=source, dst_ref=target, send_sem=send_sem.at[slot], recv_sem=recv_sem.at[slot],
            device_id=device, device_id_type=pl.DeviceIdType.MESH,
        )

    to_south = link(moved_ref, north_buf, 0, {"lat": south})
    to_north_row = link(moved_ref, south_buf, 1, {"lat": north})
    wall = link(north_ref, wall_buf, 2, {"lat": north})
    edges = [link(west_out, west_buf, 3, {"lon": east}), link(east_out, east_buf, 4, {"lon": west})]
    for copy in edges:
        copy.start()

    odd = lax.rem(lat, 2) == 1

    @pl.when(jnp.logical_and(odd, inside_north))
    def _():
        to_north_row.start()
        wall.start()

    @pl.when(inside_south)
    def _():
        to_south.start()

    @pl.when(jnp.logical_and(jnp.logical_not(odd), inside_north))
    def _():
        to_north_row.start()
        wall.start()

    @pl.when(jnp.logical_not(inside_north))
    def _():
        north_buf[...] = jnp.zeros_like(north_buf)

    @pl.when(jnp.logical_not(inside_south))
    def _():
        south_buf[...] = jnp.zeros_like(south_buf)
        wall_buf[...] = jnp.zeros_like(wall_buf)

    width = inverse.shape[1]
    place = lax.broadcasted_iota(jnp.int32, (1, width), 1)
    advected[rows:, :] = jnp.zeros((width - rows, 2 * LANES), jnp.float32)

    def product(block_ref, level, vectors):
        result = []
        for a in range(count):
            total = block_ref[a * count, 0, level] * vectors[0]
            for b in range(1, count):
                total = total + block_ref[a * count + b, 0, level] * vectors[b]
            result.append(total)
        return result

    def unit(level):
        return [jnp.where(place == b * levels + level, 1.0, 0.0).astype(jnp.float32) for b in range(count)]

    def keep(level, vectors):
        for a in range(count):
            inverse[pl.ds(a * levels + level, 1), :] = vectors[a]

    first = product(pivot_ref, 0, unit(0))
    keep(0, first)

    def forward_step(level, previous):
        coupled = product(lower_ref, level - 1, previous)
        right = [one - other for one, other in zip(unit(level), coupled)]
        current = product(pivot_ref, level, right)
        keep(level, current)
        return tuple(current)

    last = lax.fori_loop(1, levels, forward_step, tuple(first))

    def backward_step(step, following):
        level = levels - 2 - step
        coupled = product(upper_ref, level, following)
        current = [inverse[pl.ds(a * levels + level, 1), :] - coupled[a] for a in range(count)]
        keep(level, current)
        return tuple(current)

    lax.fori_loop(0, levels - 1, backward_step, last)

    for copy in edges:
        copy.wait()

    spot = lax.broadcasted_iota(jnp.int32, (rows, LANES), 1)
    shape = (count, levels, LANES)

    def upwind(speed, behind, ahead):
        return (
            jnp.maximum(speed, 0.0)[None] * behind.reshape(shape)
            + jnp.minimum(speed, 0.0)[None] * ahead.reshape(shape)
        ).reshape(rows, LANES)

    east_edge = unpack_column(east_buf[...], 0, groups)
    west_edge = unpack_column(west_buf[...], 0, groups)
    west_speed = unpack_column(west_buf[...], groups, levels // SUB)
    flux = [
        upwind(courant[0], own[0], pltpu.roll(jnp.where(spot == 0, own[1], own[0]), LANES - 1, 1)),
        upwind(courant[1], own[1], pltpu.roll(jnp.where(spot == 0, east_edge, own[1]), LANES - 1, 1)),
    ]
    from_west = [
        jnp.where(spot == 0, upwind(west_speed, west_edge, own[0]), pltpu.roll(flux[0], 1, 1)),
        pltpu.roll(jnp.where(spot == LANES - 1, flux[0], flux[1]), 1, 1),
    ]
    for half in range(2):
        base[half] = own[half] - (flux[half] - from_west[half])

    @pl.when(inside_south)
    def _():
        to_south.wait_send()
        to_north_row.wait_recv()
        wall.wait_recv()

    @pl.when(inside_north)
    def _():
        to_north_row.wait_send()
        wall.wait_send()
        to_south.wait_recv()

    for half in range(2):
        part, level_part = pl.ds(half, rows, stride=2), pl.ds(half, levels, stride=2)
        north_wall = jnp.where(lat == lat_count - 1, 0.0, north_ref[level_part, :])
        south_wall = jnp.where(lat == 0, 0.0, wall_buf[level_part, :])
        middle = moved_ref[part, :]
        to_north = upwind(north_wall, middle, north_buf[part, :])
        from_south = upwind(south_wall, south_buf[part, :], middle)
        advected[:rows, half * LANES:(half + 1) * LANES] = base[half] - (to_north - from_south)


def apply_inverse(inverse, advected, out_ref):
    solved = lax.dot_general(
        inverse[...], advected[...], (((1,), (0,)), ((), ())),
        precision=lax.Precision.HIGHEST, preferred_element_type=jnp.float32,
    )
    for half in range(2):
        out_ref[pl.ds(half, inverse.shape[0], stride=2), :] = solved[:, half * LANES:(half + 1) * LANES]


def body(fields, east_courant, north_courant, offsets, lower_blocks, pivot_inverse, upper_blocks):
    cycle_count = lax.axis_size("lon")
    band_count = lax.axis_size("lat")
    count, levels = fields.shape[:2]
    rows = count * levels
    displace = jnp.mod(offsets, cycle_count)

    def shift_by(step):
        pairs = [(place, (place + step) % cycle_count) for place in range(cycle_count)]

        def branch(block):
            return block if step == 0 else lax.ppermute(block, "lon", pairs)

        return branch

    moved = lax.switch(
        displace[0], [shift_by(step) for step in range(cycle_count)], fields.reshape(2 * rows, LANES)
    )
    width = -(-rows // 256) * 256
    vmem = pl.BlockSpec(memory_space=pltpu.VMEM)
    smem = pl.BlockSpec(memory_space=pltpu.SMEM)
    inverse, advected = pl.pallas_call(
        lambda *refs: kernel((count, levels, band_count, cycle_count), *refs),
        out_shape=(
            jax.ShapeDtypeStruct((rows, width), jnp.float32),
            jax.ShapeDtypeStruct((width, 2 * LANES), jnp.float32),
        ),
        in_specs=[vmem] * 3 + [smem] * 3,
        out_specs=(vmem, vmem),
        scratch_shapes=[
            pltpu.VMEM((2 * rows, LANES), jnp.float32),
            pltpu.VMEM((2 * rows, LANES), jnp.float32),
            pltpu.VMEM((2 * levels, LANES), jnp.float32),
            pltpu.VMEM((SUB, LANES), jnp.float32),
            pltpu.VMEM((SUB, LANES), jnp.float32),
            pltpu.VMEM((SUB, LANES), jnp.float32),
            pltpu.VMEM((SUB, LANES), jnp.float32),
            pltpu.VMEM((2, rows, LANES), jnp.float32),
            pltpu.SemaphoreType.DMA((5,)),
            pltpu.SemaphoreType.DMA((5,)),
        ],
        compiler_params=pltpu.CompilerParams(
            collective_id=0, has_side_effects=True, vmem_limit_bytes=8 * 1024 * 1024
        ),
    )(
        moved,
        east_courant.reshape(2 * levels, LANES),
        north_courant.reshape(2 * levels, LANES),
        jnp.swapaxes(lower_blocks, 2, 3).reshape(count * count, 1, levels - 1),
        jnp.swapaxes(pivot_inverse, 2, 3).reshape(count * count, 1, levels),
        jnp.swapaxes(upper_blocks, 2, 3).reshape(count * count, 1, levels - 1),
    )
    solved = pl.pallas_call(
        apply_inverse,
        out_shape=jax.ShapeDtypeStruct((2 * rows, LANES), jnp.float32),
        in_specs=[vmem] * 2,
        out_specs=vmem,
        compiler_params=pltpu.CompilerParams(vmem_limit_bytes=8 * 1024 * 1024),
    )(inverse, advected)
    return solved.reshape(fields.shape)


def solution(mesh):
    in_specs = (
        P(None, None, "lat", "lon"),
        P(None, "lat", "lon"),
        P(None, "lat", "lon"),
        P("lat"),
        P(None, None, None, "lat"),
        P(None, None, None, "lat"),
        P(None, None, None, "lat"),
    )
    out_specs = P(None, None, "lat", "lon")
    return jax.shard_map(body, mesh=mesh, in_specs=in_specs, out_specs=out_specs, check_vma=False)
```
